512 devices in a mesh: dp: 64 (over z, y_hi, core), tensor: 8 (over x, y_lo).
Axes of the slice: x: 4, y: 4 (y_hi: 2, y_lo: 2; y = y_hi * 2 + y_lo), z: 16, core: 2. Of those that a mesh axis runs over, the one named last changes fastest.
Arguments:
- context: bfloat16 [8192, 4096], P('dp', 'tensor'), may hold values from -6 to 6
- out_weight: bfloat16 [4096, 2048], P('tensor'), may hold values from -0.09375 to 0.09375
- residual_in: float32 [8192, 2048], P('dp', 'tensor')
- norm_gain: float32 [2048], P('tensor'), may hold values from 0.1 to 1.9
- expert_ids: int32 [8192, 8], P('dp'), may hold values from 0 to 63, all different within a row; in each aligned block of 128 rows (0 to 127, 128 to 255, ...) at most 24 rows name the same one
- expert_gates: float32 [8192, 8], P('dp'), may hold values from 0.05 to 1
- w_gate: bfloat16 [64, 1536, 2048], P('dp', 'tensor'), may hold values from -0.125 to 0.125
- w_up: bfloat16 [64, 1536, 2048], P('dp', 'tensor'), may hold values from -0.125 to 0.125
- w_down: bfloat16 [64, 1536, 2048], P('dp', None, 'tensor'), may hold values from -0.15625 to 0.15625
Outputs:
- attended: float32 [8192, 2048], P('dp', 'tensor')
- expert_mix: bfloat16 [8192, 2048], P('dp', 'tensor')
The draws below stay inside these ranges and needn't reach their ends.
Inputs may be any that keep to these rules, and one draw needn't show every extreme that they name: `expert_ids`: each token names 8 different experts. The 128 tokens of one index of dp (aligned blocks of rows) name any one expert at most 24 times, a bound that some block reaches.
All inputs are finite; a program needn't handle non-finite values.
Results may differ from the reference program's by a relative error of at most 0.0071.
Values may be sent and summed in bfloat16 or wider, within the bound.
A program may use at most 64 MiB of HBM per device.

```python
import math
import jax
import jax.numpy as jnp
import numpy as np
from jax import lax

D = 2048
HEADS = 32
HEAD_DIM = 128
FF = 1536
TOPK = 8
TOK_DEV = 128
EXPERTS = 64
TOKENS = 8192
CAP = 24
N_DP = 64


def draw_residual_in(key, part):
    key_base, key_cols, key_rows = jax.random.split(key, 3)
    column = jnp.arange(D, dtype=jnp.float32) / D
    col_scale = 10.0 ** column * jnp.exp(jax.random.uniform(key_cols, (D,), jnp.float32, -0.35, 0.35))
    base_draw = jax.random.normal(key_base, (TOKENS, D), jnp.float32)
    row_scale = 10.0 ** jax.random.uniform(key_rows, (TOKENS, 1), jnp.float32, 0.0, 1.0)
    return (0.3 * base_draw * col_scale * row_scale).astype(jnp.float32)


def steps_of(stream_key, shape, cuts, least, largest):
    level = 1.0
    for axis_at, parts in cuts:
        steps = jax.random.uniform(jax.random.fold_in(jax.random.fold_in(stream_key, 6), axis_at), (parts,), jnp.float32, least / len(cuts), largest / len(cuts))
        level = level * jnp.repeat(jnp.exp(steps), shape[axis_at] // parts).reshape((-1,) + (1,) * (len(shape) - 1 - axis_at))
    return level


def assign_block(rng, own, number, rows, amount, top, reach, slope):
    order = jax.random.permutation(rng, amount)
    packed, usual = load_shares(amount, rows * top, reach, slope, True), load_shares(amount, rows * top, reach, slope, False)
    places = jnp.arange(amount)

    def named(sizes, turn):
        used = int((sizes > 0).sum())
        fixed = max(1, used // 4)
        moved = fixed + (places - fixed + turn * (used - fixed)) % max(1, amount - fixed)
        return jnp.zeros((amount,), jnp.int32).at[order[jnp.where(places < fixed, places, moved)]].set(jnp.asarray(sizes, jnp.int32))

    sizes = jnp.where(number % 4 == 0, named(packed, number // 4), named(usual, number - number // 4 - 1))
    mixed = jax.random.permutation(jax.random.fold_in(own, 3), amount)
    source_of, taker = mixed[0:amount // 2 * 2:2], mixed[1:amount // 2 * 2:2]
    margin = jnp.minimum(sizes[source_of] - 1, reach - sizes[taker]) // 2
    margin = jnp.where((source_of == order[0]) | (taker == order[0]) | (sizes[taker] == 0), 0, jnp.maximum(margin, 0))
    moved = jax.random.randint(jax.random.fold_in(own, 4), (amount // 2,), 0, 1 << 20) % (margin + 1)
    sizes = sizes.at[source_of].add(-moved).at[taker].add(moved)
    items = jnp.searchsorted(jnp.cumsum(sizes), jnp.arange(rows * top), side="right").astype(jnp.int32)
    listing = items.reshape(top, rows).T
    listing = listing[jax.random.permutation(jax.random.fold_in(own, 1), rows)]
    turn = jax.random.randint(jax.random.fold_in(own, 2), (rows, 1), 0, top)
    return jnp.take_along_axis(listing, (jnp.arange(top)[None, :] + turn) % top, axis=1)


def load_shares(count, total, bound, skew, full):
    weights = [(1 << 20) // math.isqrt(rank ** skew) + 1 for rank in range(1, count + 1)]
    largest = bound if full else min(bound, max(-(-total // count), total * weights[0] // sum(weights)))
    least = 1 if total - largest >= count - 1 else 0
    counts, surplus = [largest] + [least] * (count - 1), total - largest - least * (count - 1)
    while surplus > 0:
        candidates = [i for i in range(1, count) if counts[i] < largest] or [i for i in range(1, count) if counts[i] < bound]
        whole, left = sum([weights[i] for i in candidates]), surplus
        for i in candidates:
            extra = min(bound - counts[i], max(1, left * weights[i] // whole), surplus)
            counts[i] = counts[i] + extra
            surplus = surplus - extra
    return np.array(counts)


def scatter_about(rng, shape, spread, reach, cuts=(), kind=jnp.bfloat16):
    gain = steps_of(rng, shape, cuts, -0.22, 0.18) if cuts else 1.0
    result = jax.random.normal(rng, shape, jnp.float32) * spread * gain
    return jnp.minimum(jnp.maximum(result, -reach), reach).astype(kind)


def setup_inputs(seed: int = 0) -> dict:
    key_list = jax.random.split(jax.random.key(seed), 10)
    context = scatter_about(key_list[0], (TOKENS, HEADS * HEAD_DIM), 1.0, 6.0, ((0, 64), (1, 8)))
    out_weight = scatter_about(key_list[1], (HEADS * HEAD_DIM, D), (HEADS * HEAD_DIM) ** -0.5, 0.09375, ((0, 8),))
    residual_in = draw_residual_in(jax.random.fold_in(key_list[9], 71), 0)
    norm_gain = jnp.clip(1.0 + 0.18 * jax.random.normal(key_list[3], (D,), jnp.float32), 0.1, 1.9)
    expert_ids_keys = jax.random.split(jax.random.fold_in(key_list[4], 1), TOKENS // TOK_DEV)
    expert_ids_turns = jax.random.permutation(jax.random.fold_in(key_list[4], 3), TOKENS // TOK_DEV)
    expert_ids = jax.vmap(lambda own, number: assign_block(jax.random.fold_in(key_list[4], 2), own, number, TOK_DEV, EXPERTS, TOPK, CAP, 2))(expert_ids_keys, expert_ids_turns).reshape((TOKENS, TOPK))
    expert_gates = jnp.clip(jnp.exp(math.log(1.0) - 2.9957323 * jax.random.uniform(key_list[5], (TOKENS, TOPK), jnp.float32) ** steps_of(key_list[5], (TOKENS, TOPK), ((0, 64),), -0.2, 0.2)), 0.05, 1.0)
    w_gate = scatter_about(key_list[6], (EXPERTS, FF, D), D ** -0.5, 0.125, ((0, 64), (1, 8)))
    w_up = scatter_about(key_list[7], (EXPERTS, FF, D), D ** -0.5, 0.125, ((0, 64), (1, 8)))
    w_down = scatter_about(key_list[8], (EXPERTS, FF, D), FF ** -0.5, 0.15625, ((0, 64), (2, 8)))
    return {"context": context, "out_weight": out_weight, "residual_in": residual_in, "norm_gain": norm_gain, "expert_ids": expert_ids, "expert_gates": expert_gates, "w_gate": w_gate, "w_up": w_up, "w_down": w_down}


epsilon = 1e-06

def reference(context, out_weight, residual_in, norm_gain, expert_ids, expert_gates, w_gate, w_up, w_down):
    projected = jnp.dot(context, out_weight, preferred_element_type=jnp.float32)
    attended = residual_in + projected
    mean_square = lax.optimization_barrier(jnp.mean(attended * attended, axis=1, keepdims=True))
    normed = (attended * lax.rsqrt(mean_square + epsilon) * norm_gain).astype(jnp.bfloat16)
    num_pairs = expert_ids.shape[0] * TOPK
    flat_ids = expert_ids.reshape(-1).astype(jnp.int32)
    sorted_pairs = jnp.argsort(flat_ids, stable=True).astype(jnp.int32)
    expert_load = lax.optimization_barrier(jnp.sum((flat_ids[:, None] == jnp.arange(EXPERTS, dtype=jnp.int32)[None, :]).astype(jnp.int32), axis=0))
    expert_start = (jnp.cumsum(expert_load) - expert_load).astype(jnp.int32)
    rank = jnp.zeros((num_pairs,), jnp.int32).at[sorted_pairs].set(jnp.arange(num_pairs, dtype=jnp.int32) - expert_start[flat_ids[sorted_pairs]])
    slot_count = N_DP * CAP

    def per_expert(expert):
        slot_range = jnp.arange(slot_count, dtype=jnp.int32)
        sorted_at = jnp.minimum(expert_start[expert] + slot_range, num_pairs - 1)
        routed_rows = normed[sorted_pairs[sorted_at] // TOPK]
        gate_val = jnp.dot(routed_rows, w_gate[expert].T, preferred_element_type=jnp.float32)
        up_val = jnp.dot(routed_rows, w_up[expert].T, preferred_element_type=jnp.float32)
        activation = (jax.nn.silu(gate_val) * up_val).astype(jnp.bfloat16)
        summed_out = jnp.dot(activation, w_down[expert], preferred_element_type=jnp.float32)
        return summed_out.astype(jnp.bfloat16)
    expert_out = lax.map(per_expert, jnp.arange(EXPERTS, dtype=jnp.int32))
    picked = expert_out[flat_ids, rank].reshape(expert_ids.shape[0], TOPK, D).astype(jnp.float32)
    weights = expert_gates / lax.optimization_barrier(jnp.sum(expert_gates, axis=1, keepdims=True))
    expert_mix = lax.optimization_barrier(jnp.sum(weights[:, :, None] * picked, axis=1)).astype(jnp.bfloat16)
    return (attended, expert_mix)
```

```python
import functools

import jax
import jax.numpy as jnp
from jax import lax
from jax.experimental import pallas as pl
from jax.experimental.pallas import tpu as pltpu
from jax.sharding import PartitionSpec as P

epsilon = 1e-06
MESH = pl.DeviceIdType.MESH
NX, NY = 4, 2
CHUNKS = 4


def neighbours():
    me = lax.axis_index("tensor")
    x, y = me // NY, lax.rem(me, NY)
    at = lambda dx, dy: lax.rem(x + dx, NX) * NY + lax.rem(y + dy, NY)
    owners = [me, at(0, 1), at(3, 0), at(1, 0), at(2, 0), at(3, 1), at(1, 1), at(2, 1)]
    return owners, at(0, 1), at(1, 0), at(3, 0)


class Gather:
    def __init__(self, own, view, sends, recvs, partner, right, left):
        kinds = [
            (own, view(1, None), partner),
            (own, view(2, None), right),
            (own, view(3, None), left),
            (view(2, 0), view(4, 0), right),
            (view(3, 1), view(4, 1), left),
            (view(1, None), view(5, None), right),
            (view(1, None), view(6, None), left),
            (view(4, None), view(7, None), partner),
        ]
        self.copies = [
            pltpu.make_async_remote_copy(
                src_ref=src, dst_ref=dst, send_sem=sends.at[k], recv_sem=recvs.at[k],
                device_id={"tensor": to}, device_id_type=MESH,
            )
            for k, (src, dst, to) in enumerate(kinds)
        ]

    def start(self):
        for k in (1, 2, 0):
            self.copies[k].start()

    def relay(self):
        c = self.copies
        c[1].wait_recv()
        c[3].start()
        c[2].wait_recv()
        c[4].start()
        c[0].wait_recv()
        c[5].start()
        c[6].start()

    def cross(self):
        c = self.copies
        c[3].wait_recv()
        c[4].wait_recv()
        c[7].start()

    def arrive(self):
        for k in (5, 6, 7):
            self.copies[k].wait_recv()

    def drain(self):
        for c in self.copies:
            c.wait_send()


def expert_kernel(
    x_ref, gate_ref, up_ref, down_ref, out_ref,
    xg, ag, wcat, wd1, wd2, own_sem, x_send, x_recv, a_send, a_recv,
):
    rows, width = x_ref.shape
    hidden = gate_ref.shape[0]
    rest = hidden - 128
    size = rows // CHUNKS
    packed = size + size // 2
    owners, partner, right, left = neighbours()

    barrier = pltpu.get_barrier_semaphore()
    for other in (partner, right, left):
        pl.semaphore_signal(barrier, inc=1, device_id={"tensor": other}, device_id_type=MESH)
    pl.semaphore_wait(barrier, 3)

    def x_view(c):
        def view(slot, half):
            start, count = c * size, size
            if half is not None:
                start, count = start + half * (size // 2), size // 2
            return xg.at[pl.ds(start, count), pl.ds(slot * width, width)]
        return view

    def a_view(c):
        def view(slot, half):
            start, count = c * packed, packed
            if half is not None:
                start, count = start + half * (packed // 2), packed // 2
            return ag.at[pl.ds(start, count), pl.ds(slot * 128, 128)]
        return view

    gx = [
        Gather(x_ref.at[pl.ds(c * size, size)], x_view(c), x_send.at[c], x_recv.at[c], partner, right, left)
        for c in range(CHUNKS)
    ]
    ga = [
        Gather(a_view(c)(0, None), a_view(c), a_send.at[c], a_recv.at[c], partner, right, left)
        for c in range(CHUNKS)
    ]
    for g in gx:
        g.start()
    own = pltpu.make_async_copy(x_ref, xg.at[:, pl.ds(0, width)], own_sem)
    own.start()

    wcat[...] = jnp.zeros_like(wcat)
    wd2[...] = jnp.zeros_like(wd2)
    for slot, owner in enumerate(owners):
        cols = pl.ds(pl.multiple_of(owner * width, width), width)
        here = pl.ds(slot * width, width)
        wcat[0:hidden, here] = gate_ref[:, cols]
        wcat[256:256 + hidden, here] = up_ref[:, cols]
        base = owner * hidden
        wd1[pl.ds(slot * 128, 128), :] = down_ref[pl.ds(pl.multiple_of(base, 64), 128), :]
        tail = down_ref[pl.ds(pl.multiple_of(base + 128, 64), rest), :]
        wd2[pl.ds(slot * 128, rest), 0:width] = tail
        wd2[pl.ds(slot * 128 + rest, rest), width:2 * width] = tail
    own.wait()

    def gate_up(c):
        h = lax.dot_general(
            xg[pl.ds(c * size, size), :], wcat[...], (((1,), (1,)), ((), ())),
            preferred_element_type=jnp.float32,
        )
        gate, up = h[:, 0:256], h[:, 256:512]
        act = gate / (1.0 + jnp.exp(-gate)) * up
        tail = act[:, 128:256]
        tail = tail[0:size // 2] + pltpu.roll(tail[size // 2:size], 64, 1)
        ag[pl.ds(c * packed, size), 0:128] = act[:, 0:128].astype(jnp.bfloat16)
        ag[pl.ds(c * packed + size, size // 2), 0:128] = tail.astype(jnp.bfloat16)

    def down(c):
        first = jnp.dot(ag[pl.ds(c * packed, size), :], wd1[...], preferred_element_type=jnp.float32)
        second = jnp.dot(
            ag[pl.ds(c * packed + size, size // 2), :], wd2[...], preferred_element_type=jnp.float32
        )
        half = size // 2
        out_ref[pl.ds(c * size, half), :] = (first[0:half] + second[:, 0:width]).astype(jnp.bfloat16)
        out_ref[pl.ds(c * size + half, half), :] = (first[half:] + second[:, width:]).astype(jnp.bfloat16)

    for step in range(CHUNKS + 5):
        at = lambda lag: step - lag if 0 <= step - lag < CHUNKS else None
        if at(0) is not None:
            gx[at(0)].relay()
        if at(1) is not None:
            gx[at(1)].cross()
        if at(2) is not None:
            gx[at(2)].arrive()
            gate_up(at(2))
            ga[at(2)].start()
        if at(3) is not None:
            ga[at(3)].relay()
        if at(4) is not None:
            ga[at(4)].cross()
        if at(5) is not None:
            ga[at(5)].arrive()
            down(at(5))
    for g in gx + ga:
        g.drain()


def experts(x, gate, up, down):
    rows, width = x.shape
    size = rows // CHUNKS
    packed = size + size // 2
    vmem = pl.BlockSpec(memory_space=pltpu.VMEM)
    return pl.pallas_call(
        expert_kernel,
        out_shape=jax.ShapeDtypeStruct((rows, width), jnp.bfloat16),
        in_specs=[vmem] * 4,
        out_specs=vmem,
        scratch_shapes=[
            pltpu.VMEM((rows, 8 * width), jnp.bfloat16),
            pltpu.VMEM((CHUNKS * packed, 8 * 128), jnp.bfloat16),
            pltpu.VMEM((512, 8 * width), jnp.bfloat16),
            pltpu.VMEM((8 * 128, width), jnp.bfloat16),
            pltpu.VMEM((8 * 128, 2 * width), jnp.bfloat16),
            pltpu.SemaphoreType.DMA,
            pltpu.SemaphoreType.DMA((CHUNKS, 8)),
            pltpu.SemaphoreType.DMA((CHUNKS, 8)),
            pltpu.SemaphoreType.DMA((CHUNKS, 8)),
            pltpu.SemaphoreType.DMA((CHUNKS, 8)),
        ],
        compiler_params=pltpu.CompilerParams(
            collective_id=0, has_side_effects=True, vmem_limit_bytes=48 * 1024 * 1024
        ),
    )(x, gate, up, down)


def local(
    context, out_weight, residual_in, norm_gain, expert_ids, expert_gates, w_gate, w_up, w_down
):
    num_tokens, width_local = residual_in.shape
    top_count = expert_ids.shape[1]
    num_experts = w_gate.shape[0] * lax.axis_size("dp")
    capacity = max(2, 3 * num_tokens * top_count // (2 * num_experts))
    slots = num_experts * capacity
    summed_proj = lax.psum_scatter(
        jnp.einsum("th,hd->dt", context, out_weight, preferred_element_type=jnp.float32),
        "tensor",
        scatter_dimension=0,
        tiled=True,
    )
    weights = expert_gates / jnp.sum(expert_gates, axis=1, keepdims=True)
    named = expert_ids[:, :, None] == jnp.arange(num_experts, dtype=jnp.int32)[None, None, :]
    member = jnp.any(named, axis=1)
    weight = jnp.sum(jnp.where(named, weights[:, :, None], 0.0), axis=1)
    order = jnp.arange(num_tokens, dtype=jnp.int32)
    before = (order[None, :] < order[:, None]).astype(jnp.bfloat16)
    rank = jnp.dot(before, member.astype(jnp.bfloat16), preferred_element_type=jnp.float32)
    rank = jnp.where(member, rank, -1.0).astype(jnp.bfloat16)
    slot = jnp.arange(slots, dtype=jnp.int32)
    spread = (slot[None, :] // capacity == jnp.arange(num_experts, dtype=jnp.int32)[:, None]).astype(
        jnp.bfloat16
    )
    high = lax.reduce_precision(weight, 8, 7)
    low = weight - high
    stacked = jnp.concatenate([rank, high.astype(jnp.bfloat16), low.astype(jnp.bfloat16)], axis=0)
    wide = jnp.dot(stacked, spread, preferred_element_type=jnp.float32)
    place = wide[:num_tokens] == (slot % capacity).astype(jnp.float32)[None, :]
    mix_high = jnp.where(place, wide[num_tokens:2 * num_tokens], 0.0).astype(jnp.bfloat16)
    mix_low = jnp.where(place, wide[2 * num_tokens:], 0.0).astype(jnp.bfloat16)
    place = place.astype(jnp.bfloat16)

    attended = residual_in + summed_proj.T
    squares = lax.psum(jnp.sum(attended * attended, axis=1), "tensor")
    full_width = width_local * lax.axis_size("tensor")
    scaling = lax.rsqrt(squares / full_width + epsilon)
    normed = (attended * scaling[:, None] * norm_gain).astype(jnp.bfloat16)

    outgoing = lax.dot_general(
        place, normed, (((0,), (0,)), ((), ())), preferred_element_type=jnp.float32
    ).astype(jnp.bfloat16)
    outgoing = outgoing.reshape(num_experts, capacity, width_local)
    received = lax.all_to_all(outgoing, "dp", split_axis=0, concat_axis=0, tiled=True)
    result = experts(received.reshape(slots, width_local), w_gate[0], w_up[0], w_down[0])
    result = result.reshape(num_experts, capacity, width_local)
    returned = lax.all_to_all(result, "dp", split_axis=0, concat_axis=0, tiled=True)
    flat_back = returned.reshape(slots, width_local)
    mixed = jnp.dot(mix_high, flat_back, preferred_element_type=jnp.float32)
    mixed = mixed + jnp.dot(mix_low, flat_back, preferred_element_type=jnp.float32)
    return (attended, mixed.astype(jnp.bfloat16))


def solution(mesh):
    return jax.shard_map(
        local,
        mesh=mesh,
        in_specs=(
            P("dp", "tensor"),
            P("tensor", None),
            P("dp", "tensor"),
            P("tensor"),
            P("dp", None),
            P("dp", None),
            P("dp", "tensor", None),
            P("dp", "tensor", None),
            P("dp", None, "tensor"),
        ),
        out_specs=(P("dp", "tensor"), P("dp", "tensor")),
        check_vma=False,
    )
```

```python
import functools

import jax
import jax.numpy as jnp
from jax import lax
from jax.experimental import pallas as pl
from jax.experimental.pallas import tpu as pltpu
from jax.sharding import PartitionSpec as P

epsilon = 1e-06
MESH = pl.DeviceIdType.MESH
NX, NY, NZ, DP = 4, 2, 16, 64
CHUNKS = 4


def neighbours():
    me = lax.axis_index("tensor")
    x, y = me // NY, lax.rem(me, NY)
    at = lambda dx, dy: lax.rem(x + dx, NX) * NY + lax.rem(y + dy, NY)
    owners = [me, at(0, 1), at(3, 0), at(1, 0), at(2, 0), at(3, 1), at(1, 1), at(2, 1)]
    return owners, at(0, 1), at(1, 0), at(3, 0)


class Gather:
    def __init__(self, own, view, sends, recvs, partner, right, left):
        kinds = [
            (own, view(1, None), partner),
            (own, view(2, None), right),
            (own, view(3, None), left),
            (view(2, 0), view(4, 0), right),
            (view(3, 1), view(4, 1), left),
            (view(1, None), view(5, None), right),
            (view(1, None), view(6, None), left),
            (view(4, None), view(7, None), partner),
        ]
        self.copies = [
            pltpu.make_async_remote_copy(
                src_ref=src, dst_ref=dst, send_sem=sends.at[k], recv_sem=recvs.at[k],
                device_id={"tensor": to}, device_id_type=MESH,
            )
            for k, (src, dst, to) in enumerate(kinds)
        ]

    def start(self):
        for k in (1, 2, 0):
            self.copies[k].start()

    def relay(self):
        c = self.copies
        c[1].wait_recv()
        c[3].start()
        c[2].wait_recv()
        c[4].start()
        c[0].wait_recv()
        c[5].start()
        c[6].start()

    def cross(self):
        c = self.copies
        c[3].wait_recv()
        c[4].wait_recv()
        c[7].start()

    def arrive(self):
        for k in (5, 6, 7):
            self.copies[k].wait_recv()

    def drain(self):
        for c in self.copies:
            c.wait_send()


def peer(p, sign):
    dp = lax.axis_index("dp")
    i, a, b = p // 4, lax.rem(p // 2, 2), lax.rem(p, 2)
    odd = lax.rem(i, 2)
    dz = odd * ((i + 1) // 2) + (1 - odd) * lax.rem(NZ - i // 2, NZ)
    z = lax.rem(dp // 4 + NZ + sign * dz, NZ)
    return z * 4 + lax.rem(lax.rem(dp // 2, 2) + a, 2) * 2 + lax.rem(lax.rem(dp, 2) + b, 2)


def expert_kernel(
    x_ref, high_ref, low_ref, gate_ref, up_ref, down_ref, out_ref,
    xg, ag, wlo, whi, wd1, wd2, ob, ret, own_sem, d_send, d_recv, r_send, r_recv,
    x_send, x_recv, a_send, a_recv,
):
    slots = x_ref.shape[0]
    block = slots // DP
    row = block // 2
    hidden = gate_ref.shape[0]
    rest = hidden - 128
    per = DP // CHUNKS
    xsize = per * block
    size = per * row
    packed = size + size // 2
    owners, partner, right, left = neighbours()
    me = lax.axis_index("dp")

    barrier = pltpu.get_barrier_semaphore()
    for other in (partner, right, left):
        pl.semaphore_signal(barrier, inc=1, device_id={"tensor": other}, device_id_type=MESH)

    @pl.loop(1, DP)
    def _(p):
        pl.semaphore_signal(barrier, inc=1, device_id={"dp": peer(p, 1)}, device_id_type=MESH)

    wlo[...] = jnp.zeros_like(wlo)
    whi[...] = jnp.zeros_like(whi)
    wd2[...] = jnp.zeros_like(wd2)
    for slot, owner in enumerate(owners):
        here = pl.ds(slot * 128, 128)
        for part, w in enumerate((wlo, whi)):
            cols = pl.ds(pl.multiple_of(owner * 256 + part * 128, 128), 128)
            w[0:hidden, here] = gate_ref[:, cols]
            w[256:256 + hidden, here] = up_ref[:, cols]
        base = owner * hidden
        wd1[here, :] = down_ref[pl.ds(pl.multiple_of(base, 64), 128), :]
        tail = down_ref[pl.ds(pl.multiple_of(base + 128, 64), rest), :]
        wd2[pl.ds(slot * 128, rest), 0:256] = tail
        wd2[pl.ds(slot * 128 + rest, rest), 256:512] = tail
    pl.semaphore_wait(barrier, 3 + DP - 1)

    def rows_at(p):
        return pl.ds(pl.multiple_of(p * block, 16), block)

    def send(p):
        to = peer(p, -1)
        return pltpu.make_async_remote_copy(
            src_ref=x_ref.at[rows_at(to)], dst_ref=xg.at[rows_at(p), pl.ds(0, 128)],
            send_sem=d_send, recv_sem=d_recv.at[p // per], device_id={"dp": to}, device_id_type=MESH,
        )

    def give_back(p):
        to = peer(p, 1)
        return pltpu.make_async_remote_copy(
            src_ref=ob.at[rows_at(p)], dst_ref=ret.at[rows_at(me)],
            send_sem=r_send, recv_sem=r_recv, device_id={"dp": to}, device_id_type=MESH,
        )

    @pl.loop(1, DP)
    def _(p):
        send(p).start()

    own = pltpu.make_async_copy(x_ref.at[rows_at(me)], xg.at[pl.ds(0, block), pl.ds(0, 128)], own_sem.at[0])
    own.start()
    own_back = pltpu.make_async_copy(ob.at[pl.ds(0, block)], ret.at[rows_at(me)], own_sem.at[1])

    def wait_for(ref, sem):
        pltpu.make_async_copy(ref, ref, sem).wait()

    def received(c):
        if c == 0:
            wait_for(xg.at[pl.ds(block, xsize - block), pl.ds(0, 128)], d_recv.at[0])
            own.wait()
        else:
            wait_for(xg.at[pl.ds(c * xsize, xsize), pl.ds(0, 128)], d_recv.at[c])

    def view_of(buf, rows, c):
        def view(slot, half):
            start, count = c * rows, rows
            if half is not None:
                start, count = start + half * (rows // 2), rows // 2
            return buf.at[pl.ds(start, count), pl.ds(slot * 128, 128)]
        return view

    def gathers(buf, rows, sends, recvs):
        views = [view_of(buf, rows, c) for c in range(CHUNKS)]
        return [
            Gather(v(0, None), v, sends.at[c], recvs.at[c], partner, right, left)
            for c, v in enumerate(views)
        ]

    gx = gathers(xg, xsize, x_send, x_recv)
    ga = gathers(ag, packed, a_send, a_recv)

    def times(x, w):
        h = lax.dot_general(x, w, (((1,), (1,)), ((), ())), preferred_element_type=jnp.float32)
        return h.reshape(per, block, 512)

    def gate_up(c):
        x = xg[pl.ds(c * xsize, xsize), :]
        h = times(x, wlo[...])[:, 0:row] + times(x, whi[...])[:, row:]
        h = h.reshape(size, 512)
        gate, up = h[:, 0:256], h[:, 256:512]
        act = gate / (1.0 + jnp.exp(-gate)) * up
        tail = act[:, 128:256]
        tail = tail[0:size // 2] + pltpu.roll(tail[size // 2:size], 64, 1)
        ag[pl.ds(c * packed, size), 0:128] = act[:, 0:128].astype(jnp.bfloat16)
        ag[pl.ds(c * packed + size, size // 2), 0:128] = tail.astype(jnp.bfloat16)

    def down(c):
        first = jnp.dot(ag[pl.ds(c * packed, size), :], wd1[...], preferred_element_type=jnp.float32)
        second = jnp.dot(
            ag[pl.ds(c * packed + size, size // 2), :], wd2[...], preferred_element_type=jnp.float32
        )
        second = jnp.concatenate([second[:, 0:256], second[:, 256:512]], axis=0)
        result = (first + second).reshape(per, row, 256)
        result = jnp.concatenate([result[:, :, 0:128], result[:, :, 128:256]], axis=1)
        ob[pl.ds(c * xsize, xsize), :] = result.reshape(xsize, 128).astype(jnp.bfloat16)
        if c == 0:
            own_back.start()

        @pl.loop(max(1, c * per), (c + 1) * per)
        def _(p):
            give_back(p).start()

    for step in range(CHUNKS + 6):
        at = lambda lag: step - lag if 0 <= step - lag < CHUNKS else None
        if at(0) is not None:
            received(at(0))
            gx[at(0)].start()
        if at(1) is not None:
            gx[at(1)].relay()
        if at(2) is not None:
            gx[at(2)].cross()
        if at(3) is not None:
            gx[at(3)].arrive()
            gate_up(at(3))
            ga[at(3)].start()
        if at(4) is not None:
            ga[at(4)].relay()
        if at(5) is not None:
            ga[at(5)].cross()
        if at(6) is not None:
            ga[at(6)].arrive()
            down(at(6))
    own_back.wait()
    others = pl.ds(0, slots - block)
    wait_for(ret.at[others], r_recv)

    back = ret[...]
    lower = lax.rem(lax.broadcasted_iota(jnp.int32, (slots, 128), 0), block) < row
    zero = jnp.zeros_like(back)
    back = jnp.concatenate([jnp.where(lower, back, zero), jnp.where(lower, zero, back)], axis=1)
    mixed = jnp.dot(high_ref[...], back, preferred_element_type=jnp.float32)
    mixed = mixed + jnp.dot(low_ref[...], back, preferred_element_type=jnp.float32)
    out_ref[...] = mixed.astype(jnp.bfloat16)

    wait_for(x_ref.at[others], d_send)
    wait_for(ob.at[others], r_send)
    for g in gx + ga:
        g.drain()


def experts(x, high, low, gate, up, down):
    slots = x.shape[0]
    packed = slots // 2 * 3 // 2
    vmem = pl.BlockSpec(memory_space=pltpu.VMEM)
    dma = pltpu.SemaphoreType.DMA
    return pl.pallas_call(
        expert_kernel,
        out_shape=jax.ShapeDtypeStruct((high.shape[0], 256), jnp.bfloat16),
        in_specs=[vmem] * 6,
        out_specs=vmem,
        scratch_shapes=[
            pltpu.VMEM((slots, 8 * 128), jnp.bfloat16),
            pltpu.VMEM((packed, 8 * 128), jnp.bfloat16),
            pltpu.VMEM((512, 8 * 128), jnp.bfloat16),
            pltpu.VMEM((512, 8 * 128), jnp.bfloat16),
            pltpu.VMEM((8 * 128, 256), jnp.bfloat16),
            pltpu.VMEM((8 * 128, 512), jnp.bfloat16),
            pltpu.VMEM((slots, 128), jnp.bfloat16),
            pltpu.VMEM((slots, 128), jnp.bfloat16),
            dma((2,)), dma, dma((CHUNKS,)), dma, dma,
            dma((CHUNKS, 8)), dma((CHUNKS, 8)), dma((CHUNKS, 8)), dma((CHUNKS, 8)),
        ],
        compiler_params=pltpu.CompilerParams(
            collective_id=0, has_side_effects=True, vmem_limit_bytes=56 * 1024 * 1024
        ),
    )(x, high, low, gate, up, down)


def local(
    context, out_weight, residual_in, norm_gain, expert_ids, expert_gates, w_gate, w_up, w_down
):
    num_tokens, width_local = residual_in.shape
    top_count = expert_ids.shape[1]
    num_experts = w_gate.shape[0] * lax.axis_size("dp")
    capacity = max(2, 3 * num_tokens * top_count // (2 * num_experts))
    summed_proj = lax.psum_scatter(
        jnp.einsum("th,hd->dt", context, out_weight, preferred_element_type=jnp.float32),
        "tensor",
        scatter_dimension=0,
        tiled=True,
    )
    weights = expert_gates / jnp.sum(expert_gates, axis=1, keepdims=True)
    named = expert_ids[:, :, None] == jnp.arange(num_experts, dtype=jnp.int32)[None, None, :]
    member = jnp.any(named, axis=1)
    weight = jnp.sum(jnp.where(named, weights[:, :, None], 0.0), axis=1)
    order = jnp.arange(num_tokens, dtype=jnp.int32)
    before = (order[None, :] < order[:, None]).astype(jnp.bfloat16)
    rank = jnp.dot(before, member.astype(jnp.bfloat16), preferred_element_type=jnp.float32)
    rank = jnp.where(member, rank, -1.0).astype(jnp.bfloat16)
    block = 2 * capacity
    slot = jnp.arange(num_experts * block, dtype=jnp.int32)
    spread = (slot[None, :] // block == jnp.arange(num_experts, dtype=jnp.int32)[:, None]).astype(
        jnp.bfloat16
    )
    high = lax.reduce_precision(weight, 8, 7)
    low = weight - high
    stacked = jnp.concatenate([rank, high.astype(jnp.bfloat16), low.astype(jnp.bfloat16)], axis=0)
    wide = jnp.dot(stacked, spread, preferred_element_type=jnp.float32)
    place = wide[:num_tokens] == (slot % capacity).astype(jnp.float32)[None, :]
    mix_high = jnp.where(place, wide[num_tokens:2 * num_tokens], 0.0).astype(jnp.bfloat16)
    mix_low = jnp.where(place, wide[2 * num_tokens:], 0.0).astype(jnp.bfloat16)
    place = place.astype(jnp.bfloat16)

    attended = residual_in + summed_proj.T
    squares = lax.psum(jnp.sum(attended * attended, axis=1), "tensor")
    full_width = width_local * lax.axis_size("tensor")
    scaling = lax.rsqrt(squares / full_width + epsilon)
    normed = (attended * scaling[:, None] * norm_gain).astype(jnp.bfloat16)

    outgoing = lax.dot_general(
        place, normed, (((0,), (0,)), ((), ())), preferred_element_type=jnp.float32
    )
    lower = (slot % block < capacity)[:, None]
    outgoing = jnp.where(lower, outgoing[:, :128], outgoing[:, 128:]).astype(jnp.bfloat16)
    mixed = experts(outgoing, mix_high, mix_low, w_gate[0], w_up[0], w_down[0])
    return (attended, mixed)


def solution(mesh):
    return jax.shard_map(
        local,
        mesh=mesh,
        in_specs=(
            P("dp", "tensor"),
            P("tensor", None),
            P("dp", "tensor"),
            P("tensor"),
            P("dp", None),
            P("dp", None),
            P("dp", "tensor", None),
            P("dp", "tensor", None),
            P("dp", None, "tensor"),
        ),
        out_specs=(P("dp", "tensor"), P("dp", "tensor")),
        check_vma=False,
    )
```

```python
import functools

import jax
import jax.numpy as jnp
from jax import lax
from jax.experimental import pallas as pl
from jax.experimental.pallas import tpu as pltpu
from jax.sharding import PartitionSpec as P

epsilon = 1e-06
MESH = pl.DeviceIdType.MESH
NX, NY, NZ, DP = 4, 2, 16, 64
CHUNKS = 4


def neighbours():
    me = lax.axis_index("tensor")
    x, y = me // NY, lax.rem(me, NY)
    at = lambda dx, dy: lax.rem(x + dx, NX) * NY + lax.rem(y + dy, NY)
    owners = [me, at(0, 1), at(3, 0), at(1, 0), at(2, 0), at(3, 1), at(1, 1), at(2, 1)]
    return owners, at(0, 1), at(1, 0), at(3, 0)


class Gather:
    def __init__(self, own, view, sends, recvs, partner, right, left):
        kinds = [
            (own, view(1, None), partner),
            (own, view(2, None), right),
            (own, view(3, None), left),
            (view(2, 0), view(4, 0), right),
            (view(3, 1), view(4, 1), left),
            (view(1, None), view(5, None), right),
            (view(1, None), view(6, None), left),
            (view(4, None), view(7, None), partner),
        ]
        self.copies = [
            pltpu.make_async_remote_copy(
                src_ref=src, dst_ref=dst, send_sem=sends.at[k], recv_sem=recvs.at[k],
                device_id={"tensor": to}, device_id_type=MESH,
            )
            for k, (src, dst, to) in enumerate(kinds)
        ]

    def start(self):
        for k in (1, 2, 0):
            self.copies[k].start()

    def relay(self):
        c = self.copies
        c[1].wait_recv()
        c[3].start()
        c[2].wait_recv()
        c[4].start()
        c[0].wait_recv()
        c[5].start()
        c[6].start()

    def cross(self):
        c = self.copies
        c[3].wait_recv()
        c[4].wait_recv()
        c[7].start()

    def arrive(self):
        for k in (5, 6, 7):
            self.copies[k].wait_recv()

    def drain(self):
        for c in self.copies:
            c.wait_send()


def peer(p, sign):
    dp = lax.axis_index("dp")
    i, a, b = p // 4, lax.rem(p // 2, 2), lax.rem(p, 2)
    odd = lax.rem(i, 2)
    dz = odd * ((i + 1) // 2) + (1 - odd) * lax.rem(NZ - i // 2, NZ)
    z = lax.rem(dp // 4 + NZ + sign * dz, NZ)
    return z * 4 + lax.rem(lax.rem(dp // 2, 2) + a, 2) * 2 + lax.rem(lax.rem(dp, 2) + b, 2)


def block_kernel(
    context_ref, proj_ref, residual_ref, gain_ref, ids_ref, gates_ref, gate_ref, up_ref, down_ref,
    attended_ref, out_ref,
    ps, pr, sq, x_ref, place_ref, high_ref, low_ref, xg, ag, wlo, whi, wd1, wd2, ob, ret,
    p_send, p_recv, s_send, s_recv, own_sem, d_send, d_recv, r_send, r_recv,
    x_send, x_recv, a_send, a_recv,
):
    slots = x_ref.shape[0]
    block = slots // DP
    row = block // 2
    tokens, width = residual_ref.shape
    hidden = gate_ref.shape[0]
    rest = hidden - 128
    per = DP // CHUNKS
    xsize = per * block
    size = per * row
    packed = size + size // 2
    owners, partner, right, left = neighbours()
    me = lax.axis_index("dp")

    barrier = pltpu.get_barrier_semaphore()
    for other in owners[1:]:
        pl.semaphore_signal(barrier, inc=1, device_id={"tensor": other}, device_id_type=MESH)

    @pl.loop(1, DP)
    def _(p):
        pl.semaphore_signal(barrier, inc=1, device_id={"dp": peer(p, 1)}, device_id_type=MESH)

    def columns(slot):
        return pl.ds(pl.multiple_of(owners[slot] * width, width), width)

    def project(slot):
        return jnp.dot(context_ref[...], proj_ref[:, columns(slot)], preferred_element_type=jnp.float32)

    def to_all(src, dst, sends, recvs):
        return {
            k: pltpu.make_async_remote_copy(
                src_ref=src(k), dst_ref=dst(k), send_sem=sends.at[k], recv_sem=recvs.at[k],
                device_id={"tensor": owners[k]}, device_id_type=MESH,
            )
            for k in (7, 4, 5, 6, 2, 3, 1)
        }

    partials = to_all(lambda k: ps.at[k], lambda k: pr.at[k], p_send, p_recv)
    for k in partials:
        ps[k] = project(k).astype(jnp.bfloat16)
    pl.semaphore_wait(barrier, 7 + DP - 1)
    for k in partials:
        partials[k].start()
    total = residual_ref[...] + project(0)

    wlo[...] = jnp.zeros_like(wlo)
    whi[...] = jnp.zeros_like(whi)
    wd2[...] = jnp.zeros_like(wd2)
    for slot, owner in enumerate(owners):
        here = pl.ds(slot * 128, 128)
        for part, w in enumerate((wlo, whi)):
            cols = pl.ds(pl.multiple_of(owner * 256 + part * 128, 128), 128)
            w[0:hidden, here] = gate_ref[:, cols]
            w[256:256 + hidden, here] = up_ref[:, cols]
        base = owner * hidden
        wd1[here, :] = down_ref[pl.ds(pl.multiple_of(base, 64), 128), :]
        tail = down_ref[pl.ds(pl.multiple_of(base + 128, 64), rest), :]
        wd2[pl.ds(slot * 128, rest), 0:256] = tail
        wd2[pl.ds(slot * 128 + rest, rest), 256:512] = tail

    gates = gates_ref[...]
    weights = gates / jnp.sum(gates, axis=1, keepdims=True)
    ids = ids_ref[...]
    expert = lax.broadcasted_iota(jnp.int32, (tokens, DP), 1)
    member = jnp.zeros((tokens, DP), jnp.float32)
    weight = jnp.zeros((tokens, DP), jnp.float32)
    for k in range(ids.shape[1]):
        named = ids[:, k:k + 1] == expert
        member = jnp.where(named, 1.0, member)
        weight = jnp.where(named, weights[:, k:k + 1], weight)
    before = jnp.where(
        lax.broadcasted_iota(jnp.int32, (tokens, tokens), 1)
        < lax.broadcasted_iota(jnp.int32, (tokens, tokens), 0),
        1.0, 0.0,
    ).astype(jnp.bfloat16)
    rank = jnp.dot(before, member.astype(jnp.bfloat16), preferred_element_type=jnp.float32)
    rank = jnp.where(member > 0.5, rank, -1.0)
    slot_at = lax.broadcasted_iota(jnp.int32, (DP, slots), 1)
    start = lax.broadcasted_iota(jnp.int32, (DP, slots), 0) * block
    within = (slot_at >= start) & (slot_at < start + block)
    spread = jnp.where(within, 1.0, 0.0).astype(jnp.bfloat16)
    inside = jnp.sum(jnp.where(within, slot_at - start, 0).astype(jnp.float32), axis=0, keepdims=True)
    inside = jnp.where(inside >= row, inside - row, inside)

    def spread_out(v):
        return jnp.dot(v.astype(jnp.bfloat16), spread, preferred_element_type=jnp.float32)

    place = spread_out(rank) == inside
    high = weight.astype(jnp.bfloat16).astype(jnp.float32)
    high_ref[...] = jnp.where(place, spread_out(high), 0.0).astype(jnp.bfloat16)
    low_ref[...] = jnp.where(place, spread_out(weight - high), 0.0).astype(jnp.bfloat16)
    place_ref[...] = jnp.where(place, 1.0, 0.0).T.astype(jnp.bfloat16)

    for k in reversed(list(partials)):
        partials[k].wait_recv()
        total = total + pr[k].astype(jnp.float32)
    attended_ref[...] = total
    squares = jnp.sum(total * total, axis=1, keepdims=True)
    sq[0] = jnp.broadcast_to(squares, (tokens, 128)).T[0:8]
    sums = to_all(lambda k: sq.at[0], lambda k: sq.at[k], s_send, s_recv)
    for k in sums:
        sums[k].start()
    for k in sums:
        sums[k].wait_recv()
    squares = sq[0]
    for k in range(1, 8):
        squares = squares + sq[k]
    squares = jnp.broadcast_to(squares[0:1], (128, tokens)).T[:, 0:1]
    scaling = lax.rsqrt(squares / (width * 8) + epsilon)
    normed = (total * scaling * gain_ref[...]).astype(jnp.bfloat16)

    lower = lax.rem(lax.broadcasted_iota(jnp.int32, (slots, 128), 0), block) < row
    rows = jnp.dot(place_ref[...], normed, preferred_element_type=jnp.float32)
    x_ref[...] = jnp.where(lower, rows[:, 0:128], rows[:, 128:256]).astype(jnp.bfloat16)

    def rows_at(p):
        return pl.ds(pl.multiple_of(p * block, 16), block)

    def send(p):
        to = peer(p, -1)
        return pltpu.make_async_remote_copy(
            src_ref=x_ref.at[rows_at(to)], dst_ref=xg.at[rows_at(p), pl.ds(0, 128)],
            send_sem=d_send, recv_sem=d_recv.at[p // per], device_id={"dp": to}, device_id_type=MESH,
        )

    def give_back(p):
        to = peer(p, 1)
        return pltpu.make_async_remote_copy(
            src_ref=ob.at[rows_at(p)], dst_ref=ret.at[rows_at(me)],
            send_sem=r_send, recv_sem=r_recv, device_id={"dp": to}, device_id_type=MESH,
        )

    @pl.loop(1, DP)
    def _(p):
        send(p).start()

    own = pltpu.make_async_copy(x_ref.at[rows_at(me)], xg.at[pl.ds(0, block), pl.ds(0, 128)], own_sem.at[0])
    own.start()
    own_back = pltpu.make_async_copy(ob.at[pl.ds(0, block)], ret.at[rows_at(me)], own_sem.at[1])

    def wait_for(ref, sem):
        pltpu.make_async_copy(ref, ref, sem).wait()

    def received(c):
        if c == 0:
            wait_for(xg.at[pl.ds(block, xsize - block), pl.ds(0, 128)], d_recv.at[0])
            own.wait()
        else:
            wait_for(xg.at[pl.ds(c * xsize, xsize), pl.ds(0, 128)], d_recv.at[c])

    def view_of(buf, rows, c):
        def view(slot, half):
            start, count = c * rows, rows
            if half is not None:
                start, count = start + half * (rows // 2), rows // 2
            return buf.at[pl.ds(start, count), pl.ds(slot * 128, 128)]
        return view

    def gathers(buf, rows, sends, recvs):
        views = [view_of(buf, rows, c) for c in range(CHUNKS)]
        return [
            Gather(v(0, None), v, sends.at[c], recvs.at[c], partner, right, left)
            for c, v in enumerate(views)
        ]

    gx = gathers(xg, xsize, x_send, x_recv)
    ga = gathers(ag, packed, a_send, a_recv)

    def times(x, w):
        h = lax.dot_general(x, w, (((1,), (1,)), ((), ())), preferred_element_type=jnp.float32)
        return h.reshape(per, block, 512)

    def gate_up(c):
        x = xg[pl.ds(c * xsize, xsize), :]
        h = times(x, wlo[...])[:, 0:row] + times(x, whi[...])[:, row:]
        h = h.reshape(size, 512)
        gate, up = h[:, 0:256], h[:, 256:512]
        act = gate / (1.0 + jnp.exp(-gate)) * up
        tail = act[:, 128:256]
        tail = tail[0:size // 2] + pltpu.roll(tail[size // 2:size], 64, 1)
        ag[pl.ds(c * packed, size), 0:128] = act[:, 0:128].astype(jnp.bfloat16)
        ag[pl.ds(c * packed + size, size // 2), 0:128] = tail.astype(jnp.bfloat16)

    def down(c):
        first = jnp.dot(ag[pl.ds(c * packed, size), :], wd1[...], preferred_element_type=jnp.float32)
        second = jnp.dot(
            ag[pl.ds(c * packed + size, size // 2), :], wd2[...], preferred_element_type=jnp.float32
        )
        second = jnp.concatenate([second[:, 0:256], second[:, 256:512]], axis=0)
        result = (first + second).reshape(per, row, 256)
        result = jnp.concatenate([result[:, :, 0:128], result[:, :, 128:256]], axis=1)
        ob[pl.ds(c * xsize, xsize), :] = result.reshape(xsize, 128).astype(jnp.bfloat16)
        if c == 0:
            own_back.start()

        @pl.loop(max(1, c * per), (c + 1) * per)
        def _(p):
            give_back(p).start()

    for step in range(CHUNKS + 6):
        at = lambda lag: step - lag if 0 <= step - lag < CHUNKS else None
        if at(0) is not None:
            received(at(0))
            gx[at(0)].start()
        if at(1) is not None:
            gx[at(1)].relay()
        if at(2) is not None:
            gx[at(2)].cross()
        if at(3) is not None:
            gx[at(3)].arrive()
            gate_up(at(3))
            ga[at(3)].start()
        if at(4) is not None:
            ga[at(4)].relay()
        if at(5) is not None:
            ga[at(5)].cross()
        if at(6) is not None:
            ga[at(6)].arrive()
            down(at(6))
    own_back.wait()
    others = pl.ds(0, slots - block)
    wait_for(ret.at[others], r_recv)

    back = ret[...]
    zero = jnp.zeros_like(back)
    back = jnp.concatenate([jnp.where(lower, back, zero), jnp.where(lower, zero, back)], axis=1)
    mixed = jnp.dot(high_ref[...], back, preferred_element_type=jnp.float32)
    mixed = mixed + jnp.dot(low_ref[...], back, preferred_element_type=jnp.float32)
    out_ref[...] = mixed.astype(jnp.bfloat16)

    wait_for(x_ref.at[others], d_send)
    wait_for(ob.at[others], r_send)
    for g in gx + ga:
        g.drain()
    for c in [*partials.values(), *sums.values()]:
        c.wait_send()


def local(
    context, out_weight, residual_in, norm_gain, expert_ids, expert_gates, w_gate, w_up, w_down
):
    tokens, width = residual_in.shape
    slots = 3 * tokens * expert_ids.shape[1]
    packed = slots // 2 * 3 // 2
    vmem = pl.BlockSpec(memory_space=pltpu.VMEM)
    dma = pltpu.SemaphoreType.DMA
    half = jnp.bfloat16
    return pl.pallas_call(
        block_kernel,
        out_shape=(
            jax.ShapeDtypeStruct((tokens, width), jnp.float32),
            jax.ShapeDtypeStruct((tokens, width), half),
        ),
        in_specs=[vmem] * 9,
        out_specs=(vmem, vmem),
        scratch_shapes=[
            pltpu.VMEM((8, tokens, width), half),
            pltpu.VMEM((8, tokens, width), half),
            pltpu.VMEM((8, 8, 128), jnp.float32),
            pltpu.VMEM((slots, 128), half),
            pltpu.VMEM((slots, tokens), half),
            pltpu.VMEM((tokens, slots), half),
            pltpu.VMEM((tokens, slots), half),
            pltpu.VMEM((slots, 8 * 128), half),
            pltpu.VMEM((packed, 8 * 128), half),
            pltpu.VMEM((512, 8 * 128), half),
            pltpu.VMEM((512, 8 * 128), half),
            pltpu.VMEM((8 * 128, 256), half),
            pltpu.VMEM((8 * 128, 512), half),
            pltpu.VMEM((slots, 128), half),
            pltpu.VMEM((slots, 128), half),
            dma((8,)), dma((8,)), dma((8,)), dma((8,)),
            dma((2,)), dma, dma((CHUNKS,)), dma, dma,
            dma((CHUNKS, 8)), dma((CHUNKS, 8)), dma((CHUNKS, 8)), dma((CHUNKS, 8)),
        ],
        compiler_params=pltpu.CompilerParams(
            collective_id=0, has_side_effects=True, vmem_limit_bytes=60 * 1024 * 1024
        ),
    )(
        context, out_weight, residual_in, norm_gain[None, :], expert_ids, expert_gates,
        w_gate[0], w_up[0], w_down[0],
    )


def solution(mesh):
    return jax.shard_map(
        local,
        mesh=mesh,
        in_specs=(
            P("dp", "tensor"),
            P("tensor", None),
            P("dp", "tensor"),
            P("tensor"),
            P("dp", None),
            P("dp", None),
            P("dp", "tensor", None),
            P("dp", "tensor", None),
            P("dp", None, "tensor"),
        ),
        out_specs=(P("dp", "tensor"), P("dp", "tensor")),
        check_vma=False,
    )
```

```python
import functools

import jax
import jax.numpy as jnp
from jax import lax
from jax.experimental import pallas as pl
from jax.experimental.pallas import tpu as pltpu
from jax.sharding import PartitionSpec as P

epsilon = 1e-06
MESH = pl.DeviceIdType.MESH
NX, NY, NZ, DP = 4, 2, 16, 64
CHUNKS = 8


def neighbours():
    me = lax.axis_index("tensor")
    x, y = me // NY, lax.rem(me, NY)
    at = lambda dx, dy: lax.rem(x + dx, NX) * NY + lax.rem(y + dy, NY)
    owners = [me, at(0, 1), at(3, 0), at(1, 0), at(2, 0), at(3, 1), at(1, 1), at(2, 1)]
    return owners, at(0, 1), at(1, 0), at(3, 0)


class Gather:
    def __init__(self, own, view, sends, recvs, partner, right, left):
        kinds = [
            (own, view(1, None), partner),
            (own, view(2, None), right),
            (own, view(3, None), left),
            (view(2, 0), view(4, 0), right),
            (view(3, 1), view(4, 1), left),
            (view(1, None), view(5, None), right),
            (view(1, None), view(6, None), left),
            (view(4, None), view(7, None), partner),
        ]
        self.copies = [
            pltpu.make_async_remote_copy(
                src_ref=src, dst_ref=dst, send_sem=sends.at[k], recv_sem=recvs.at[k],
                device_id={"tensor": to}, device_id_type=MESH,
            )
            for k, (src, dst, to) in enumerate(kinds)
        ]

    def start(self):
        for k in (1, 2, 0):
            self.copies[k].start()

    def relay(self):
        c = self.copies
        c[1].wait_recv()
        c[3].start()
        c[2].wait_recv()
        c[4].start()
        c[0].wait_recv()
        c[5].start()
        c[6].start()

    def cross(self):
        c = self.copies
        c[3].wait_recv()
        c[4].wait_recv()
        c[7].start()

    def arrive(self):
        for k in (5, 6, 7):
            self.copies[k].wait_recv()

    def drain(self):
        for c in self.copies:
            c.wait_send()


ORDER = (0, 1, 4, 12, 8, 9, 7, 10, 6, 11, 5, 13, 3, 14, 2, 15)


def peer(dz, q):
    dp = lax.axis_index("dp")
    z = lax.rem(dp // 4 + dz, NZ)
    return z * 4 + lax.rem(lax.rem(dp // 2, 2) + q // 2, 2) * 2 + lax.rem(lax.rem(dp, 2) + lax.rem(q, 2), 2)


def each_peer(body, first=0, last=NZ):
    for i in range(first, last):
        @pl.loop(1 if i == 0 else 0, 4)
        def _(q):
            body(4 * i + q, peer(ORDER[i], q), peer(NZ - ORDER[i], q))


def block_kernel(
    context_ref, proj_ref, residual_ref, gain_ref, ids_ref, gates_ref, gate_ref, up_ref, down_ref,
    attended_ref, out_ref,
    ps, pr, sq, x_ref, place_ref, high_ref, low_ref, xg, ag, wlo, whi, wd1, wd2, ob, ret,
    p_send, p_recv, s_send, s_recv, own_sem, d_send, d_recv, r_send, r_recv,
    x_send, x_recv, a_send, a_recv,
):
    slots = x_ref.shape[0]
    block = slots // DP
    row = block // 2
    tokens, width = residual_ref.shape
    hidden = gate_ref.shape[0]
    rest = hidden - 128
    per = DP // CHUNKS
    xsize = per * block
    size = per * row
    packed = size + size // 2
    owners, partner, right, left = neighbours()
    me = lax.axis_index("dp")

    barrier = pltpu.get_barrier_semaphore()
    for other in owners[1:]:
        pl.semaphore_signal(barrier, inc=1, device_id={"tensor": other}, device_id_type=MESH)

    @pl.loop(1, DP)
    def _(p):
        pl.semaphore_signal(barrier, inc=1, device_id={"dp": lax.rem(me + p, DP)}, device_id_type=MESH)

    def columns(slot):
        return pl.ds(pl.multiple_of(owners[slot] * width, width), width)

    def project(slot):
        return jnp.dot(context_ref[...], proj_ref[:, columns(slot)], preferred_element_type=jnp.float32)

    def to_all(src, dst, sends, recvs):
        return {
            k: pltpu.make_async_remote_copy(
                src_ref=src(k), dst_ref=dst(k), send_sem=sends.at[k], recv_sem=recvs.at[k],
                device_id={"tensor": owners[k]}, device_id_type=MESH,
            )
            for k in (7, 4, 5, 6, 2, 3, 1)
        }

    partials = to_all(lambda k: ps.at[k], lambda k: pr.at[k], p_send, p_recv)
    for k in partials:
        ps[k] = project(k).astype(jnp.bfloat16)
    pl.semaphore_wait(barrier, 7 + DP - 1)
    for k in partials:
        partials[k].start()
    total = residual_ref[...] + project(0)

    gates = gates_ref[...]
    weights = (gates / jnp.sum(gates, axis=0, keepdims=True)).T
    ids = ids_ref[...].astype(jnp.float32).T
    expert = lax.broadcasted_iota(jnp.int32, (tokens, DP), 1).astype(jnp.float32)
    member = jnp.zeros((tokens, DP), jnp.float32)
    weight = jnp.zeros((tokens, DP), jnp.float32)
    for k in range(ids.shape[1]):
        named = ids[:, k:k + 1] == expert
        member = jnp.where(named, 1.0, member)
        weight = jnp.where(named, weights[:, k:k + 1], weight)
    before = jnp.where(
        lax.broadcasted_iota(jnp.int32, (tokens, tokens), 1)
        < lax.broadcasted_iota(jnp.int32, (tokens, tokens), 0),
        1.0, 0.0,
    ).astype(jnp.bfloat16)
    rank = jnp.dot(before, member.astype(jnp.bfloat16), preferred_element_type=jnp.float32)
    rank = jnp.where(member > 0.5, rank, -1.0)
    slot_at = lax.broadcasted_iota(jnp.int32, (DP, slots), 1)
    start = lax.broadcasted_iota(jnp.int32, (DP, slots), 0) * block
    within = (slot_at >= start) & (slot_at < start + block)
    spread = jnp.where(within, 1.0, 0.0).astype(jnp.bfloat16)
    inside = jnp.sum(jnp.where(within, slot_at - start, 0).astype(jnp.float32), axis=0, keepdims=True)
    inside = jnp.where(inside >= row, inside - row, inside)

    def spread_out(v):
        return jnp.dot(v.astype(jnp.bfloat16), spread, preferred_element_type=jnp.float32)

    place = spread_out(rank) == inside
    place = jnp.where(place, 1.0, 0.0)
    high_ref[...] = place.astype(jnp.bfloat16)
    place_ref[...] = place.T.astype(jnp.bfloat16)

    def mix_matrices():
        place = high_ref[...].astype(jnp.float32)
        high = weight.astype(jnp.bfloat16).astype(jnp.float32)
        high_ref[...] = (place * spread_out(high)).astype(jnp.bfloat16)
        low_ref[...] = (place * spread_out(weight - high)).astype(jnp.bfloat16)

    for k in reversed(list(partials)):
        partials[k].wait_recv()
        total = total + pr[k].astype(jnp.float32)
    attended_ref[...] = total
    squares = jnp.sum(total * total, axis=1, keepdims=True)
    sq[0] = jnp.broadcast_to(squares, (tokens, 128)).T[0:8]
    sums = to_all(lambda k: sq.at[0], lambda k: sq.at[k], s_send, s_recv)
    for k in sums:
        sums[k].start()
    for k in sums:
        sums[k].wait_recv()
    squares = sq[0]
    for k in range(1, 8):
        squares = squares + sq[k]
    squares = jnp.broadcast_to(squares[0:1], (128, tokens)).T[:, 0:1]
    scaling = lax.rsqrt(squares / (width * 8) + epsilon)
    normed = (total * scaling * gain_ref[...]).astype(jnp.bfloat16)

    lower = lax.rem(lax.broadcasted_iota(jnp.int32, (slots, 128), 0), block) < row
    rows = jnp.dot(place_ref[...], normed, preferred_element_type=jnp.float32)
    x_ref[...] = jnp.where(lower, rows[:, 0:128], rows[:, 128:256]).astype(jnp.bfloat16)

    def rows_at(p):
        return pl.ds(pl.multiple_of(p * block, 16), block)

    def send(p, _, to):
        pltpu.make_async_remote_copy(
            src_ref=x_ref.at[rows_at(to)], dst_ref=xg.at[rows_at(p), pl.ds(0, 128)],
            send_sem=d_send, recv_sem=d_recv.at[p // per], device_id={"dp": to}, device_id_type=MESH,
        ).start()

    def give_back(p, to, _):
        pltpu.make_async_remote_copy(
            src_ref=ob.at[rows_at(p)], dst_ref=ret.at[rows_at(me)],
            send_sem=r_send, recv_sem=r_recv, device_id={"dp": to}, device_id_type=MESH,
        ).start()

    each_peer(send)
    own = pltpu.make_async_copy(x_ref.at[rows_at(me)], xg.at[pl.ds(0, block), pl.ds(0, 128)], own_sem.at[0])
    own.start()
    own_back = pltpu.make_async_copy(ob.at[pl.ds(0, block)], ret.at[rows_at(me)], own_sem.at[1])

    def wait_for(ref, sem):
        pltpu.make_async_copy(ref, ref, sem).wait()

    def received(c):
        if c == 0:
            wait_for(xg.at[pl.ds(block, xsize - block), pl.ds(0, 128)], d_recv.at[0])
            own.wait()
        else:
            wait_for(xg.at[pl.ds(c * xsize, xsize), pl.ds(0, 128)], d_recv.at[c])

    def view_of(buf, rows, c):
        def view(slot, half):
            start, count = c * rows, rows
            if half is not None:
                start, count = start + half * (rows // 2), rows // 2
            return buf.at[pl.ds(start, count), pl.ds(slot * 128, 128)]
        return view

    def gathers(buf, rows, sends, recvs):
        views = [view_of(buf, rows, c) for c in range(CHUNKS)]
        return [
            Gather(v(0, None), v, sends.at[c], recvs.at[c], partner, right, left)
            for c, v in enumerate(views)
        ]

    gx = gathers(xg, xsize, x_send, x_recv)
    ga = gathers(ag, packed, a_send, a_recv)

    def times(x, w):
        h = lax.dot_general(x, w, (((1,), (1,)), ((), ())), preferred_element_type=jnp.float32)
        return h.reshape(per, block, 512)

    def gate_up(c):
        x = xg[pl.ds(c * xsize, xsize), :]
        h = times(x, wlo[...])[:, 0:row] + times(x, whi[...])[:, row:]
        h = h.reshape(size, 512)
        gate, up = h[:, 0:256], h[:, 256:512]
        act = gate / (1.0 + jnp.exp(-gate)) * up
        tail = act[:, 128:256]
        tail = tail[0:size // 2] + pltpu.roll(tail[size // 2:size], 64, 1)
        ag[pl.ds(c * packed, size), 0:128] = act[:, 0:128].astype(jnp.bfloat16)
        ag[pl.ds(c * packed + size, size // 2), 0:128] = tail.astype(jnp.bfloat16)

    def down(c):
        first = jnp.dot(ag[pl.ds(c * packed, size), :], wd1[...], preferred_element_type=jnp.float32)
        second = jnp.dot(
            ag[pl.ds(c * packed + size, size // 2), :], wd2[...], preferred_element_type=jnp.float32
        )
        second = jnp.concatenate([second[:, 0:256], second[:, 256:512]], axis=0)
        result = (first + second).reshape(per, row, 256)
        result = jnp.concatenate([result[:, :, 0:128], result[:, :, 128:256]], axis=1)
        ob[pl.ds(c * xsize, xsize), :] = result.reshape(xsize, 128).astype(jnp.bfloat16)
        if c == 0:
            own_back.start()

        each_peer(give_back, c * per // 4, (c + 1) * per // 4)

    def arrange_weights():
        wlo[...] = jnp.zeros_like(wlo)
        whi[...] = jnp.zeros_like(whi)
        wd2[...] = jnp.zeros_like(wd2)
        for slot, owner in enumerate(owners):
            here = pl.ds(slot * 128, 128)
            for part, w in enumerate((wlo, whi)):
                cols = pl.ds(pl.multiple_of(owner * 256 + part * 128, 128), 128)
                w[0:hidden, here] = gate_ref[:, cols]
                w[256:256 + hidden, here] = up_ref[:, cols]
            base = owner * hidden
            wd1[here, :] = down_ref[pl.ds(pl.multiple_of(base, 64), 128), :]
            tail = down_ref[pl.ds(pl.multiple_of(base + 128, 64), rest), :]
            wd2[pl.ds(slot * 128, rest), 0:256] = tail
            wd2[pl.ds(slot * 128 + rest, rest), 256:512] = tail

    for step in range(CHUNKS + 6):
        at = lambda lag: step - lag if 0 <= step - lag < CHUNKS else None
        if at(0) is not None:
            received(at(0))
            gx[at(0)].start()
        if at(1) is not None:
            gx[at(1)].relay()
        if step == 1:
            arrange_weights()
        if step == 6:
            mix_matrices()
        if at(2) is not None:
            gx[at(2)].cross()
        if at(3) is not None:
            gx[at(3)].arrive()
            gate_up(at(3))
            ga[at(3)].start()
        if at(4) is not None:
            ga[at(4)].relay()
        if at(5) is not None:
            ga[at(5)].cross()
        if at(6) is not None:
            ga[at(6)].arrive()
            down(at(6))
    own_back.wait()
    others = pl.ds(0, slots - block)
    wait_for(ret.at[others], r_recv)

    back = ret[...]
    zero = jnp.zeros_like(back)
    back = jnp.concatenate([jnp.where(lower, back, zero), jnp.where(lower, zero, back)], axis=1)
    mixed = jnp.dot(high_ref[...], back, preferred_element_type=jnp.float32)
    mixed = mixed + jnp.dot(low_ref[...], back, preferred_element_type=jnp.float32)
    out_ref[...] = mixed.astype(jnp.bfloat16)

    wait_for(x_ref.at[others], d_send)
    wait_for(ob.at[others], r_send)
    for g in gx + ga:
        g.drain()
    for c in [*partials.values(), *sums.values()]:
        c.wait_send()


def local(
    context, out_weight, residual_in, norm_gain, expert_ids, expert_gates, w_gate, w_up, w_down
):
    tokens, width = residual_in.shape
    slots = 3 * tokens * expert_ids.shape[1]
    packed = slots // 2 * 3 // 2
    vmem = pl.BlockSpec(memory_space=pltpu.VMEM)
    dma = pltpu.SemaphoreType.DMA
    half = jnp.bfloat16
    return pl.pallas_call(
        block_kernel,
        out_shape=(
            jax.ShapeDtypeStruct((tokens, width), jnp.float32),
            jax.ShapeDtypeStruct((tokens, width), half),
        ),
        in_specs=[vmem] * 9,
        out_specs=(vmem, vmem),
        scratch_shapes=[
            pltpu.VMEM((8, tokens, width), half),
            pltpu.VMEM((8, tokens, width), half),
            pltpu.VMEM((8, 8, 128), jnp.float32),
            pltpu.VMEM((slots, 128), half),
            pltpu.VMEM((slots, tokens), half),
            pltpu.VMEM((tokens, slots), half),
            pltpu.VMEM((tokens, slots), half),
            pltpu.VMEM((slots, 8 * 128), half),
            pltpu.VMEM((packed, 8 * 128), half),
            pltpu.VMEM((512, 8 * 128), half),
            pltpu.VMEM((512, 8 * 128), half),
            pltpu.VMEM((8 * 128, 256), half),
            pltpu.VMEM((8 * 128, 512), half),
            pltpu.VMEM((slots, 128), half),
            pltpu.VMEM((slots, 128), half),
            dma((8,)), dma((8,)), dma((8,)), dma((8,)),
            dma((2,)), dma, dma((CHUNKS,)), dma, dma,
            dma((CHUNKS, 8)), dma((CHUNKS, 8)), dma((CHUNKS, 8)), dma((CHUNKS, 8)),
        ],
        compiler_params=pltpu.CompilerParams(
            collective_id=0, has_side_effects=True, vmem_limit_bytes=60 * 1024 * 1024
        ),
    )(
        context, out_weight, residual_in, norm_gain[None, :], expert_ids.T, expert_gates.T,
        w_gate[0], w_up[0], w_down[0],
    )


def solution(mesh):
    return jax.shard_map(
        local,
        mesh=mesh,
        in_specs=(
            P("dp", "tensor"),
            P("tensor", None),
            P("dp", "tensor"),
            P("tensor"),
            P("dp", None),
            P("dp", None),
            P("dp", "tensor", None),
            P("dp", "tensor", None),
            P("dp", None, "tensor"),
        ),
        out_specs=(P("dp", "tensor"), P("dp", "tensor")),
        check_vma=False,
    )
```
